128 devices in a mesh: blk: 128 (over x, z, y, core).
Axes of the slice: x: 4, y: 4, z: 4, core: 2. Of those that a mesh axis runs over, the one named last changes fastest.
Arguments:
- locations: float32 [2, 32768], P(None, 'blk'), may hold values from 0 to 1
- neighbors: int32 [4, 256], P(None, 'blk'), may hold values from -1 to 255, as said below
- noise_precision: float32 [32768], P('blk'), may hold values from 0.5 to 4
- right_side: float32 [16, 32768], P(None, 'blk'), may hold values from -6 to 6
Outputs:
- solution: float32 [16, 32768], P(None, 'blk')
- residual: float32 [16, 32768], P(None, 'blk')
The draws below stay inside these ranges and needn't reach their ends.
Inputs may be any that keep to these rules, and one draw needn't show every extreme that they name: `neighbors`: entry [k, b] names a block that block b conditions on; the named blocks of one column are distinct and earlier than b, -1 marks an unused slot and used slots come first. Slot 0 names b - 1 for every b > 0. Among all blocks named by the columns of the 2 blocks of one device, at most one block of any other device appears, and every device but the first names one block of the device before it.
All inputs are finite; a program needn't handle non-finite values.
Results may differ from the reference program's by a relative error of at most 0.0003.
Values sent between devices are 32-bit elements; how exact they have to be, the bound alone decides.
No kernel may reach another device: no remote copies, remote signals or barrier semaphores. Data moves between devices by JAX's collectives and lax.ppermute only.
A program may use at most 64 MiB of HBM per device.

```python
import math
import jax
import jax.numpy as jnp
from jax import lax

BS = 128
KMAX = 4
RHS = 16
ITERS = 2
BLK_DEV = 2
NBLOCKS = 256
NPTS = 32768


def draw_neighbors(key, part):
    devices = NBLOCKS // BLK_DEV
    first_key = jax.random.fold_in(key, 11)
    second_key = jax.random.fold_in(key, 23)
    third_key = jax.random.fold_in(key, 37)
    blocks = jnp.arange(NBLOCKS, dtype=jnp.int32)
    device_of = blocks // BLK_DEV
    local_row = blocks % BLK_DEV
    device_list = jnp.arange(devices, dtype=jnp.int32)
    scores = jax.random.randint(first_key, (devices, devices), 0, 2 ** 20) * devices + device_list[None, :]
    scores = jnp.where(device_list[None, :] < device_list[:, None] - 1, scores, scores + 2 ** 30)
    ranked = jnp.argsort(scores, axis=1, stable=True).astype(jnp.int32)
    chosen = jax.random.randint(second_key, (devices, devices), 0, BLK_DEV)
    counts = KMAX - jax.random.randint(third_key, (NBLOCKS,), 0, 3)
    avail = jnp.maximum(device_of - 1, 0)
    remote_count = jnp.minimum(counts - 1, avail)
    slot_list = jnp.arange(1, KMAX, dtype=jnp.int32)
    position = (local_row[:, None] * (KMAX - 1) + slot_list[None, :] - 1) % jnp.maximum(avail, 1)[:, None]
    owner_dev = ranked[device_of[:, None], position]
    picked = chosen[device_of[:, None], owner_dev]
    rest_ids = jnp.where(slot_list[None, :] - 1 < remote_count[:, None], owner_dev * BLK_DEV + picked, -1)
    first_ids = jnp.where(blocks >= 1, blocks - 1, -1)
    return jnp.concatenate([first_ids[:, None], rest_ids], axis=1).T.astype(jnp.int32)


def draw_right_side(key, part):
    position = jnp.arange(NPTS, dtype=jnp.float32) / NPTS
    base_vals = jax.random.truncated_normal(key, -3.0, 3.0, (RHS, NPTS), jnp.float32)
    values = base_vals * (1.0 + 0.8 * position)[None, :]
    return values.astype(jnp.float32)


def block_scale(stream_key, shape, shards, least, high):
    level, own = 1.0, jax.random.fold_in(stream_key, 6)
    for dim, parts in shards:
        heights = jnp.exp(jax.random.uniform(jax.random.fold_in(own, dim), (parts,), jnp.float32, least / len(shards), high / len(shards)))
        level = level * jnp.repeat(heights, shape[dim] // parts).reshape([-1 if axis == dim else 1 for axis in range(len(shape))])
    return level


def setup_inputs(seed: int = 0) -> dict:
    key_of = jax.random.split(jax.random.key(seed), 5)
    return {
        "locations": jnp.clip(1.0 * jax.random.uniform(key_of[0], (2, NPTS), jnp.float32) ** block_scale(key_of[0], (2, NPTS), ((1, 128),), -0.2, 0.2), 0.0, 1.0),
        "neighbors": draw_neighbors(jax.random.fold_in(key_of[4], 71), 0),
        "noise_precision": jnp.clip(jnp.exp(math.log(4.0) - 2.0794415 * jax.random.uniform(key_of[2], (NPTS,), jnp.float32) ** block_scale(key_of[2], (NPTS,), ((0, 128),), -0.2, 0.2)), 0.5, 4.0),
        "right_side": draw_right_side(jax.random.fold_in(key_of[4], 71), 0),
    }


corr_range = 0.4
nugget = 0.2

def covariance(first_pts, second_pts):
    diff_x = first_pts[0][:, None] - second_pts[0][None, :]
    diff_y = first_pts[1][:, None] - second_pts[1][None, :]
    return jnp.exp(-jnp.sqrt(diff_x * diff_x + diff_y * diff_y) / corr_range)

def build_block(own_pts, near_pts, used_slot, noise_blk):
    width = near_pts.shape[0] * near_pts.shape[2]
    gathered = jnp.transpose(near_pts, (1, 0, 2)).reshape(2, width)
    point_mask = jnp.repeat(used_slot, near_pts.shape[2])
    eye_c = jnp.eye(width, dtype=jnp.float32)
    eye_b = jnp.eye(own_pts.shape[1], dtype=jnp.float32)
    cov_cc = covariance(gathered, gathered) * point_mask[:, None] * point_mask[None, :]
    cov_cc = cov_cc + eye_c * (nugget * point_mask + 1.0 - point_mask)[None, :]
    cov_cb = covariance(gathered, own_pts) * point_mask[:, None]
    cov_bb = covariance(own_pts, own_pts) + nugget * eye_b
    chol_c = jnp.linalg.cholesky(cov_cc)
    first = lax.linalg.triangular_solve(chol_c, cov_cb, left_side=True, lower=True)
    coefficient = lax.linalg.triangular_solve(chol_c, first, left_side=True, lower=True, transpose_a=True)
    schur = cov_bb - jnp.dot(first.T, first, precision=lax.Precision.HIGHEST)
    chol_low = jnp.linalg.cholesky(schur)
    inv_low = lax.linalg.triangular_solve(chol_low, eye_b, left_side=True, lower=True)
    factor = jnp.dot(inv_low, coefficient.T, precision=lax.Precision.HIGHEST)
    gram_blk = eye_b + jnp.dot(chol_low.T * noise_blk[None, :], chol_low, precision=lax.Precision.HIGHEST)
    chol_gram = jnp.linalg.cholesky(gram_blk)
    half_root = lax.linalg.triangular_solve(chol_gram, chol_low.T, left_side=True, lower=True)
    precond_blk = jnp.dot(half_root.T, half_root, precision=lax.Precision.HIGHEST)
    return (inv_low, factor, precond_blk)

def reference(locations, neighbors, noise_precision, right_side):
    points = jnp.transpose(locations.reshape(2, NBLOCKS, BS), (1, 0, 2))
    block_ids = neighbors.T
    in_use = block_ids >= 0
    safe_ids = jnp.where(in_use, block_ids, 0).astype(jnp.int32)
    used_slot = in_use.astype(jnp.float32)
    noise_blk = noise_precision.reshape(NBLOCKS, BS)
    near_points = points[safe_ids]

    def one_block(packed):
        return build_block(packed[0], packed[1], packed[2], packed[3])
    inv_low, factor, precond_blk = lax.map(one_block, (points, near_points, used_slot, noise_blk))
    factor_four = factor.reshape(NBLOCKS, BS, KMAX, BS)

    def operator_apply(vector):
        near_vec = vector[safe_ids]
        whitened = jnp.einsum('bij,brj->bri', inv_low, vector, precision=lax.Precision.HIGHEST)
        whitened = whitened - jnp.einsum('bikj,bkrj->bri', factor_four, near_vec, precision=lax.Precision.HIGHEST)
        own_term = jnp.einsum('bri,bij->brj', whitened, inv_low, precision=lax.Precision.HIGHEST)
        back_terms = -jnp.einsum('bri,bikj->bkrj', whitened, factor_four, precision=lax.Precision.HIGHEST)
        back_terms = back_terms * used_slot[:, :, None, None]
        returned = jax.ops.segment_sum(back_terms.reshape(NBLOCKS * KMAX, RHS, BS), safe_ids.reshape(-1), NBLOCKS)
        return own_term + returned + noise_blk[:, None, :] * vector

    def condition(vector):
        return jnp.einsum('bri,bij->brj', vector, precond_blk, precision=lax.Precision.HIGHEST)

    def inner_dot(left, right):
        return lax.optimization_barrier(jnp.sum(left * right, axis=(0, 2)))
    residual = jnp.transpose(right_side.reshape(RHS, NBLOCKS, BS), (1, 0, 2))
    solution = jnp.zeros_like(residual)
    smoothed = condition(residual)
    direction = smoothed
    res_dot = inner_dot(residual, smoothed)
    for step in range(ITERS):
        image = operator_apply(direction)
        step_size = res_dot / inner_dot(direction, image)
        solution = solution + step_size[None, :, None] * direction
        residual = residual - step_size[None, :, None] * image
        if step + 1 < ITERS:
            smoothed = condition(residual)
            new_dot = inner_dot(residual, smoothed)
            direction = smoothed + (new_dot / res_dot)[None, :, None] * direction
            res_dot = new_dot
    solution = jnp.transpose(solution, (1, 0, 2)).reshape(RHS, NPTS)
    residual = jnp.transpose(residual, (1, 0, 2)).reshape(RHS, NPTS)
    return (solution, residual)
```

```python
import jax
import jax.numpy as jnp
from jax import lax
from jax.experimental import pallas as pl
from jax.experimental.pallas import tpu as pltpu
from jax.sharding import PartitionSpec as P

BS = 128
KMAX = 4
RHS = 16
NDEV = 128
f32 = jnp.float32
HI = lax.Precision.HIGHEST
VM = pl.BlockSpec(memory_space=pltpu.VMEM)
SM = pl.BlockSpec(memory_space=pltpu.SMEM)


def call(body, shapes, n_in, scratch=(), name=None, smem=0, limit=32):
    return pl.pallas_call(
        body,
        in_specs=[SM] * smem + [VM] * (n_in - smem),
        out_specs=[VM] * len(shapes),
        out_shape=[jax.ShapeDtypeStruct(s, f32) for s in shapes],
        scratch_shapes=list(scratch),
        compiler_params=pltpu.CompilerParams(vmem_limit_bytes=limit * 2**20),
        name=name,
    )


def dg(a,b,ca,cb):
    return lax.dot_general(a,b,(((ca,),(cb,)),((),())),precision=HI,preferred_element_type=f32)
def mm(a,b): return dg(a,b,1,0)
def mm_nt(a,b): return dg(a,b,1,1)
def mm_tn(a,b): return dg(a,b,0,0)

def chol_inverse(T, ms, put, SP=32):
    lane=lax.broadcasted_iota(jnp.int32,(8,128),1)
    sub=lax.broadcasted_iota(jnp.int32,(8,128),0)
    NP=SP//8
    for s in range(0,128,SP):
        fin=[[None]*NP for _ in ms]
        R=[[T[m,s+8*q:s+8*q+8,:] for q in range(NP)] for m in ms]
        for q in range(NP):
            base=s+8*q
            inblk=(lane>=base)&(lane<base+8)
            for n in range(len(ms)):
                W=R[n][q]
                C=[jnp.broadcast_to(W[:,base+j:base+j+1],(8,128)) for j in range(8)]
                F=W
                for j in range(8):
                    at=lane==base+j; row=sub==j
                    d=jnp.broadcast_to(C[j][j:j+1],(8,128))
                    r=1.0/d
                    unit=jnp.where(at,1.0,jnp.broadcast_to(W[j:j+1],(8,128)))
                    F=jnp.where(row,unit*lax.rsqrt(d),F)
                    if q<NP-1:
                        pr=unit*r
                        W=jnp.where(row,pr,jnp.where(at,0.0,W)-C[j]*pr)
                        ls=range(j+1,8)
                    else:
                        mul=jnp.where(sub>j,C[j]*r,0.0)
                        W=jnp.where(at&(sub>j),0.0,W)-mul*unit
                        ls=range(j+1,8)
                    for l in ls:
                        e=jnp.broadcast_to(C[l][j:j+1],(8,128))*r
                        C[l]=C[l]-C[j]*e if q==NP-1 else jnp.where(row,e,C[l]-C[j]*e)
                fin[n][q]=F
                put(ms[n],base,jnp.where(lane<=sub+base,F,0.0))
                if q<NP-1:
                    Yr=[jnp.broadcast_to(W[j:j+1],(8,128)) for j in range(8)]
                    for o in range(q+1,NP):
                        A=R[n][o]
                        acc=jnp.where(inblk,0.0,A)
                        for j in range(8):
                            acc=acc-jnp.broadcast_to(A[:,base+j:base+j+1],(8,128))*Yr[j]
                        R[n][o]=acc
        if s+SP<128:
            lane2=lax.broadcasted_iota(jnp.int32,(128-s-SP,128),1)
            ins=(lane2>=s)&(lane2<s+SP)
            for n,m in enumerate(ms):
                F=jnp.concatenate(fin[n],0)
                own=s+lax.broadcasted_iota(jnp.int32,(SP,128),0)
                lf=lax.broadcasted_iota(jnp.int32,(SP,128),1)
                U=mm_tn(F,jnp.where((lf<=own)|(lf>=s+SP),F,0.0))
                T[m,s+SP:,:]=jnp.where(ins,0.0,T[m,s+SP:,:])-U[s+SP:,:]

def cov(xc,yc,xr,yr):
    dx=xc-xr; dy=yc-yr
    return jnp.exp(jnp.sqrt(dx*dx+dy*dy)*(-2.5))

def slot(nbr,k,b):
    ident=nbr[k,b]; used=ident>=0; safe=jnp.where(used,ident,0)
    return used,safe//2,safe%2

def factor_body(nbr, recv0, loc, noise, rhs, coef, g4, gd, d0, send, X, T, G):
    i0=lax.broadcasted_iota(jnp.int32,(128,128),0); i1=lax.broadcasted_iota(jnp.int32,(128,128),1)
    eye=jnp.where(i0==i1,1.0,0.0).astype(f32)
    for b in range(2):
        xs=[];ys=[];ms=[]
        for k in range(4):
            used,dev,which=slot(nbr,k,b)
            xs.append(recv0[pl.ds(5*dev+which,1),:]); ys.append(recv0[pl.ds(5*dev+which+2,1),:])
            ms.append(jnp.where(used,1.0,0.0).astype(f32))
        xs.append(loc[0:1,b*128:(b+1)*128]); ys.append(loc[1:2,b*128:(b+1)*128]); ms.append(jnp.float32(1.0))
        xt=jnp.transpose(jnp.concatenate(xs+[xs[4]]*3,0)); yt=jnp.transpose(jnp.concatenate(ys+[ys[4]]*3,0))
        for k in range(5):
            xc=jnp.broadcast_to(xt[:,k:k+1],(128,128)); yc=jnp.broadcast_to(yt[:,k:k+1],(128,128))
            for l in range(k+1):
                c=cov(xc,yc,xs[l],ys[l])
                if k<4 or l<4: c=c*(ms[k]*ms[l])
                if k==l: c=c+eye*(0.2*ms[k]+1.0-ms[k])
                X[b,k*128:(k+1)*128,l*128:(l+1)*128]=c
    T[0]=X[0,0:128,0:128]; T[1]=X[1,0:128,0:128]
    def stage(k,_):
        def put(m,row,v): G[k,m,row:row+8,:]=v
        chol_inverse(T,[0,1],put)
        for kk in range(4):
            @pl.when(k==kk)
            def _():
                lo=(kk+1)*128
                for b in range(2):
                    L=mm_nt(X[b,lo:,kk*128:lo],G[kk,b])
                    X[b,lo:,kk*128:lo]=L
                    for j in range(kk+1,5):
                        o=j*128
                        v=X[b,o:,o:o+128]-mm_nt(L[o-lo:],L[o-lo:o-lo+128])
                        if j==kk+1: T[b]=v[:128]
                        X[b,o:,o:o+128]=v
        return 0
    lax.fori_loop(0,4,stage,0)
    dn=[]
    for b in range(2):
        d=1.0/noise[0:1,b*128:(b+1)*128]; dn.append(d)
        T[2+b]=T[b]+eye*d
    def put4(m,row,v):
        if m<2: g4[m,row:row+8,:]=v
        else: gd[m-2,row:row+8,:]=v
    chol_inverse(T,[0,1,2,3],put4)
    ds=[]
    for b in range(2):
        cs=[None]*4
        for k in (3,2,1,0):
            e=X[b,512:,k*128:(k+1)*128]
            for j in range(k+1,4):
                e=e-mm(cs[j],X[b,j*128:(j+1)*128,k*128:(k+1)*128])
            cs[k]=mm(e,G[k,b])
            coef[b,:,k*128:(k+1)*128]=cs[k]
        w=rhs[:,b*128:(b+1)*128]*dn[b]
        d=w-mm(mm_nt(w,gd[b]),gd[b])*dn[b]
        d0[b]=d
        ds.append(d)
    def pack(j,_):
        flag=recv0[pl.ds(5*j+4,1),:]
        send[pl.ds(pl.multiple_of(RHS*j,RHS),RHS),:]=jnp.where(flag==1.0,ds[1],ds[0])
        return 0
    lax.fori_loop(0,NDEV,pack,0,unroll=8)


def each(n, body, unroll=8):
    def step(j, carry):
        body(j)
        return carry

    lax.fori_loop(0, n, step, 0, unroll=unroll)


def announce_body(nbr, loc, out):
    rows = jnp.concatenate(
        [loc[0:1, 0:BS], loc[0:1, BS:], loc[1:2, 0:BS], loc[1:2, BS:], jnp.full((1, BS), -1.0, f32)], 0
    )

    def put(j):
        out[pl.ds(5 * j, 5), :] = rows

    each(NDEV, put)
    for b in range(2):
        for k in range(KMAX):
            used, dev, which = slot(nbr, k, b)

            @pl.when(used)
            def _():
                out[pl.ds(5 * dev + 4, 1), :] = jnp.full((1, BS), which.astype(f32), f32)


def apply_body(rows, nbr, v, recv, coef, g4, noise, *rest):
    if rows == RHS:
        q_out, part_out, send = rest
        send[...] = jnp.zeros((NDEV * RHS, BS), f32)
    else:
        parts, q_out, send = rest
    part = jnp.zeros((RHS, BS), f32)
    backs = []
    slots = [[slot(nbr, k, b) for k in range(KMAX)] for b in range(2)]
    for b in range(2):
        near = jnp.concatenate([recv[pl.ds(pl.multiple_of(RHS * s[1], 8), RHS), :] for s in slots[b]], 1)
        own = v[b]
        t = mm_nt(own - mm_nt(near, coef[b]), g4[b])
        q = mm(t, g4[b])
        part = part + t * t + noise[0:1, b * BS : (b + 1) * BS] * own * own
        q_out[b] = q
        backs.append(-mm(q, coef[b]))
    if rows == RHS:
        part_out[...] = part
    else:
        lane = lax.broadcasted_iota(jnp.int32, (RHS, BS), 1)
        sub = lax.broadcasted_iota(jnp.int32, (RHS, BS), 0)
        z = jnp.zeros((RHS, BS), f32)
        for c, val in enumerate((parts[0], parts[1], parts[2], part)):
            z = z + jnp.where(lane == c * RHS + sub, jnp.sum(val, axis=1, keepdims=True), 0.0)
        msg = jnp.concatenate([jnp.zeros((RHS, BS), f32), jnp.sum(z, axis=0, keepdims=True)], 0)

        def put(j):
            send[pl.ds(rows * j, rows), :] = msg

        each(NDEV, put)
    for b in range(2):
        for k in range(KMAX):
            used, dev, _ = slots[b][k]

            @pl.when(used)
            def _():
                at = pl.ds(rows * dev, RHS)
                send[at, :] = send[at, :] + backs[b][:, k * BS : (k + 1) * BS]


def returned(rows, recv0, recv):
    def step(j, acc):
        flag = recv0[pl.ds(5 * j + 4, 1), :]
        msg = recv[pl.ds(rows * j, RHS), :]
        out = [a + jnp.where(flag == float(w), msg, 0.0) for w, a in enumerate(acc[:2])]
        if rows > RHS:
            out.append(acc[2] + recv[pl.ds(rows * j + RHS, 1), :])
        return tuple(out)

    init = (jnp.zeros((RHS, BS), f32), jnp.zeros((RHS, BS), f32))
    if rows > RHS:
        init = init + (jnp.zeros((1, BS), f32),)
    return lax.fori_loop(0, NDEV, step, init, unroll=8)


def middle_body(recv0, recv, q, d0, noise, rhs, gd, apart, im0, y, parts, send):
    ret = returned(RHS, recv0, recv)
    rz = jnp.zeros((RHS, BS), f32)
    bb = jnp.zeros((RHS, BS), f32)
    ys = []
    for b in range(2):
        s = slice(b * BS, (b + 1) * BS)
        d = d0[b]
        im = q[b] + ret[b] + noise[0:1, s] * d
        dn = 1.0 / noise[0:1, s]
        w = im * dn
        yb = w - mm(mm_nt(w, gd[b]), gd[b]) * dn
        im0[b] = im
        y[b] = yb
        ys.append(yb)
        bb = bb + im * yb
        rz = rz + rhs[:, s] * d
    parts[0] = rz
    parts[1] = apart[...]
    parts[2] = bb

    def put(j):
        flag = recv0[pl.ds(5 * j + 4, 1), :]
        send[pl.ds(pl.multiple_of(RHS * j, RHS), RHS), :] = jnp.where(flag == 1.0, ys[1], ys[0])

    each(NDEV, put)


def last_body(recv0, recv, q1, y, d0, im0, noise, rhs, sol, res):
    ret = returned(RHS + 1, recv0, recv)
    lane = lax.broadcasted_iota(jnp.int32, (RHS, BS), 1)
    sub = lax.broadcasted_iota(jnp.int32, (RHS, BS), 0)
    rz, a, bb, cc = [
        jnp.sum(jnp.where(lane == c * RHS + sub, ret[2], 0.0), axis=1, keepdims=True) for c in range(4)
    ]
    al0 = rz / a
    new = al0 * al0 * bb - rz
    grow = 1.0 + new / rz
    al1 = new / (al0 * al0 * cc - grow * grow * a)
    for b in range(2):
        s = slice(b * BS, (b + 1) * BS)
        w = q1[b] + ret[b] + noise[0:1, s] * y[b]
        sol[:, s] = al0 * d0[b] + al1 * (grow * d0[b] - al0 * y[b])
        res[:, s] = rhs[:, s] - al0 * im0[b] - al1 * (grow * im0[b] - al0 * w)


def per_device(locations, neighbors, noise_precision, right_side):
    noise = noise_precision.reshape(1, 2 * BS)
    blk = (2, RHS, BS)
    sq = (2, BS, BS)

    def exchange(msg, rows):
        out = lax.all_to_all(msg.reshape(NDEV, 1, rows * BS), "blk", 0, 0, tiled=True)
        return out.reshape(NDEV * rows, BS)

    (send0,) = call(announce_body, [(NDEV * 5, BS)], 2, smem=1, name="announce")(neighbors, locations)
    recv0 = exchange(send0, 5)
    coef, g4, gd, d0, send1 = call(
        factor_body,
        [(2, BS, KMAX * BS), sq, sq, blk, (NDEV * RHS, BS)],
        5,
        smem=1,
        scratch=[pltpu.VMEM((2, 640, 640), f32), pltpu.VMEM((4, BS, BS), f32), pltpu.VMEM((4, 2, BS, BS), f32)],
        name="factor",
    )(neighbors, recv0, locations, noise, right_side)
    recv1 = exchange(send1, RHS)
    q0, apart, send2 = call(
        lambda *r: apply_body(RHS, *r), [blk, (RHS, BS), (NDEV * RHS, BS)], 6, smem=1, name="apply_first"
    )(neighbors, d0, recv1, coef, g4, noise)
    recv2 = exchange(send2, RHS)
    im0, y, parts, send3 = call(
        middle_body, [blk, blk, (3, RHS, BS), (NDEV * RHS, BS)], 8, name="middle"
    )(recv0, recv2, q0, d0, noise, right_side, gd, apart)
    recv3 = exchange(send3, RHS)
    q1, send4 = call(
        lambda *r: apply_body(RHS + 1, *r), [blk, (NDEV * (RHS + 1), BS)], 7, smem=1, name="apply_second"
    )(neighbors, y, recv3, coef, g4, noise, parts)
    recv4 = exchange(send4, RHS + 1)
    return tuple(
        call(last_body, [(RHS, 2 * BS)] * 2, 8, name="last")(
            recv0, recv4, q1, y, d0, im0, noise, right_side
        )
    )


def solution(mesh):
    in_specs = (P(None, "blk"), P(None, "blk"), P("blk"), P(None, "blk"))
    out_specs = (P(None, "blk"), P(None, "blk"))
    return jax.shard_map(
        per_device, mesh=mesh, in_specs=in_specs, out_specs=out_specs, check_vma=False
    )
```

```python
import jax
import jax.numpy as jnp
from jax import lax
from jax.experimental import pallas as pl
from jax.experimental.pallas import tpu as pltpu
from jax.sharding import PartitionSpec as P

BS = 128
KMAX = 4
RHS = 16
NDEV = 128
f32 = jnp.float32
HI = lax.Precision.HIGHEST
VM = pl.BlockSpec(memory_space=pltpu.VMEM)
SM = pl.BlockSpec(memory_space=pltpu.SMEM)


def call(body, shapes, n_in, scratch=(), name=None, smem=0, limit=32):
    return pl.pallas_call(
        body,
        in_specs=[SM] * smem + [VM] * (n_in - smem),
        out_specs=[VM] * len(shapes),
        out_shape=[jax.ShapeDtypeStruct(s, f32) for s in shapes],
        scratch_shapes=list(scratch),
        compiler_params=pltpu.CompilerParams(vmem_limit_bytes=limit * 2**20),
        name=name,
    )


def dg(a,b,ca,cb):
    return lax.dot_general(a,b,(((ca,),(cb,)),((),())),precision=HI,preferred_element_type=f32)
def mm(a,b): return dg(a,b,1,0)
def mm_nt(a,b): return dg(a,b,1,1)
def mm_tn(a,b): return dg(a,b,0,0)

def chol_pieces(T, ms, put, SP=32):
    lane=lax.broadcasted_iota(jnp.int32,(8,128),1)
    sub=lax.broadcasted_iota(jnp.int32,(8,128),0)
    NP=SP//8
    for s in range(0,128,SP):
        fin=[[None]*NP for _ in ms]
        R=[[T[m,s+8*q:s+8*q+8,:] for q in range(NP)] for m in ms]
        for q in range(NP):
            base=s+8*q
            inblk=(lane>=base)&(lane<base+8)
            for n in range(len(ms)):
                W=R[n][q]
                C=[jnp.broadcast_to(jnp.sum(jnp.where(lane==base+j,W,0.0),axis=1,keepdims=True),(8,128)) for j in range(8)]
                F=W
                for j in range(8):
                    at=lane==base+j; row=sub==j
                    d=jnp.broadcast_to(C[j][j:j+1],(8,128))
                    r=1.0/d
                    unit=jnp.where(at,1.0,jnp.broadcast_to(W[j:j+1],(8,128)))
                    F=jnp.where(row,unit*lax.rsqrt(d),F)
                    if q<NP-1:
                        pr=unit*r
                        W=jnp.where(row,pr,jnp.where(at,0.0,W)-C[j]*pr)
                        ls=range(j+1,8)
                    else:
                        mul=jnp.where(sub>j,C[j]*r,0.0)
                        W=jnp.where(at&(sub>j),0.0,W)-mul*unit
                        ls=range(j+1,8)
                    for l in ls:
                        e=jnp.broadcast_to(C[l][j:j+1],(8,128))*r
                        C[l]=C[l]-C[j]*e if q==NP-1 else jnp.where(row,e,C[l]-C[j]*e)
                fin[n][q]=F
                put(ms[n],base,jnp.where(lane<=sub+base,F,0.0))
                if q<NP-1:
                    Yr=[jnp.broadcast_to(W[j:j+1],(8,128)) for j in range(8)]
                    for o in range(q+1,NP):
                        A=R[n][o]
                        acc=jnp.where(inblk,0.0,A)
                        for j in range(8):
                            acc=acc-jnp.broadcast_to(jnp.sum(jnp.where(lane==base+j,A,0.0),axis=1,keepdims=True),(8,128))*Yr[j]
                        R[n][o]=acc
            yield
        if s+SP<128:
            lane2=lax.broadcasted_iota(jnp.int32,(128-s-SP,128),1)
            ins=(lane2>=s)&(lane2<s+SP)
            for n,m in enumerate(ms):
                F=jnp.concatenate(fin[n],0)
                own=s+lax.broadcasted_iota(jnp.int32,(SP,128),0)
                lf=lax.broadcasted_iota(jnp.int32,(SP,128),1)
                F2=jnp.where((lf<=own)|(lf>=s+SP),F,0.0)
                T[m,s+SP:,:]=jnp.where(ins,0.0,T[m,s+SP:,:])-mm(jnp.transpose(F)[s+SP:],F2)
            yield

def chol_inverse(T, ms, put, fill=(), pieces=19):
    fill=list(fill)
    for i,_ in enumerate(chol_pieces(T,ms,put)):
        take=-(-len(fill)//max(pieces-i,1))
        for f in fill[:take]: f()
        fill=fill[take:]
    for f in fill: f()

def cov(xc,yc,xr,yr):
    dx=xc-xr; dy=yc-yr
    return jnp.exp(jnp.sqrt(dx*dx+dy*dy)*(-2.5))

def slot(nbr,k,b):
    ident=nbr[b,k]; used=ident>=0; safe=jnp.where(used,ident,0)
    return used,safe//2,safe%2

def factor_body(nbr_hbm, recv0, own_hbm, fac, g4, gd, d0, send, own, nbr_v, X, T, G, coef, nbr, sems):
    pairs=[(nbr_hbm,nbr),(own_hbm,own),(nbr_hbm,nbr_v)]
    copies=[pltpu.make_async_copy(a,b,sems.at[i]) for i,(a,b) in enumerate(pairs)]
    for c in copies: c.start()
    for c in copies: c.wait()
    i0=lax.broadcasted_iota(jnp.int32,(128,128),0); i1=lax.broadcasted_iota(jnp.int32,(128,128),1)
    eye=jnp.where(i0==i1,1.0,0.0).astype(f32)
    early=[]
    for b in range(2):
        xs=[];ys=[];ms=[]
        for k in range(4):
            used,dev,which=slot(nbr,k,b)
            xs.append(recv0[pl.ds(5*dev+which,1),:]); ys.append(recv0[pl.ds(5*dev+which+2,1),:])
            ms.append(jnp.where(used,1.0,0.0).astype(f32))
        xs.append(own[0:1,b*128:(b+1)*128]); ys.append(own[1:2,b*128:(b+1)*128]); ms.append(jnp.float32(1.0))
        xt=jnp.transpose(jnp.concatenate(xs+[xs[4]]*3,0)); yt=jnp.transpose(jnp.concatenate(ys+[ys[4]]*3,0))
        def block(k,l,b=b,xs=xs,ys=ys,ms=ms,xt=xt,yt=yt):
            xc=jnp.broadcast_to(xt[:,k:k+1],(128,128)); yc=jnp.broadcast_to(yt[:,k:k+1],(128,128))
            c=cov(xc,yc,xs[l],ys[l])
            if k<4 or l<4: c=c*(ms[k]*ms[l])
            if k==l: c=c+eye*(0.2*ms[k]+1.0-ms[k])
            if k==0: T[b]=c
            else: X[b,k*128:(k+1)*128,l*128:(l+1)*128]=c
        block(0,0)
        for k in range(1,5):
            for l in range(k+1):
                early.append(lambda k=k,l=l,block=block: block(k,l))
    def at(i,j): return (slice(i*128,(i+1)*128),slice(j*128,(j+1)*128))
    fill=early
    for k in range(4):
        def put(m,row,v,k=k): G[k,m,row:row+8,:]=v
        chol_inverse(T,[0,1],put,fill)
        fill=[]
        n=k+1
        for b in range(2):
            r,c=at(n,k)
            L=mm_nt(X[b,r,c],G[k,b])
            X[b,r,c]=L
            r,c=at(n,n)
            T[b]=X[b,r,c]-mm_nt(L,L)
        for b in range(2):
            def rest(b=b,k=k,n=n):
                if n<4:
                    lo=(n+1)*128
                    X[b,lo:,k*128:n*128]=mm_nt(X[b,lo:,k*128:n*128],G[k,b])
            def column(j,b=b,k=k,n=n):
                lo=max(j,n+1)*128
                c=slice(k*128,n*128)
                X[b,lo:,j*128:(j+1)*128]=X[b,lo:,j*128:(j+1)*128]-mm_nt(X[b,lo:,c],X[b,j*128:(j+1)*128,c])
            if n<4:
                fill.append(rest)
                for j in range(n,5): fill.append(lambda j=j,column=column: column(j))
    dn=[]
    for b in range(2):
        d=1.0/own[2:3,b*128:(b+1)*128]; dn.append(d)
        T[2+b]=T[b]+eye*d
    def put4(m,row,v):
        if m<2: g4[m,row:row+8,:]=v
        else: gd[m-2,row:row+8,:]=v
    for k in (3,2,1,0):
        for b in range(2):
            def term(b=b,k=k):
                X[b,512:,k*128:(k+1)*128]=X[b,512:,k*128:(k+1)*128]-mm(coef[b,:,(k+1)*128:],X[b,(k+1)*128:512,k*128:(k+1)*128])
            def close(b=b,k=k):
                coef[b,:,k*128:(k+1)*128]=mm(X[b,512:,k*128:(k+1)*128],G[k,b])
            if k<3: fill.append(term)
            fill.append(close)
    chol_inverse(T,[0,1,2,3],put4,fill)
    ds=[]
    for b in range(2):
        fac[b]=mm(g4[b],coef[b])
        w=own[8:24,b*128:(b+1)*128]*dn[b]
        d=w-mm(mm_nt(w,gd[b]),gd[b])*dn[b]
        d0[b]=d
        ds.append(d)
    def pack(j,_):
        flag=recv0[pl.ds(5*j+4,1),:]
        send[pl.ds(pl.multiple_of(RHS*j,RHS),RHS),:]=jnp.where(flag==1.0,ds[1],ds[0])
        return 0
    lax.fori_loop(0,NDEV,pack,0,unroll=8)


def each(n, body, unroll=8):
    def step(j, carry):
        body(j)
        return carry

    lax.fori_loop(0, n, step, 0, unroll=unroll)


def announce_body(nbr_hbm, loc_hbm, noise_hbm, rhs_hbm, out, own, nbr, sems):
    pairs = [(nbr_hbm, nbr), (loc_hbm, own.at[0:2]), (noise_hbm, own.at[2:3]), (rhs_hbm, own.at[8:24])]
    copies = [pltpu.make_async_copy(s, d, sems.at[i]) for i, (s, d) in enumerate(pairs)]
    own[...] = jnp.zeros((24, 2 * BS), f32)
    for c in copies:
        c.start()
    for c in copies:
        c.wait()
    loc = own[0:2, :]
    rows = jnp.concatenate(
        [loc[0:1, 0:BS], loc[0:1, BS:], loc[1:2, 0:BS], loc[1:2, BS:], jnp.full((1, BS), -1.0, f32)], 0
    )

    def put(j):
        out[pl.ds(5 * j, 5), :] = rows

    each(NDEV, put)
    for b in range(2):
        for k in range(KMAX):
            used, dev, which = slot(nbr, k, b)

            @pl.when(used)
            def _():
                out[pl.ds(5 * dev + 4, 1), :] = jnp.full((1, BS), which.astype(f32), f32)


def apply_body(rows, nbr, v, recv, fac, g4, args, *rest):
    if rows == RHS:
        q_out, part_out, send = rest
        send[...] = jnp.zeros((NDEV * RHS, BS), f32)
    else:
        parts, q_out, send = rest
    part = jnp.zeros((RHS, BS), f32)
    backs = []
    slots = [[slot(nbr, k, b) for k in range(KMAX)] for b in range(2)]
    for b in range(2):
        near = jnp.concatenate([recv[pl.ds(pl.multiple_of(RHS * s[1], 8), RHS), :] for s in slots[b]], 1)
        own = v[b]
        t = mm_nt(own, g4[b]) - mm_nt(near, fac[b])
        q = mm(t, g4[b])
        part = part + t * t + args[2:3, b * BS : (b + 1) * BS] * own * own
        q_out[b] = q
        backs.append(-mm(t, fac[b]))
    if rows == RHS:
        part_out[...] = part
    else:
        lane = lax.broadcasted_iota(jnp.int32, (RHS, BS), 1)
        sub = lax.broadcasted_iota(jnp.int32, (RHS, BS), 0)
        z = jnp.zeros((RHS, BS), f32)
        for c, val in enumerate((parts[0], parts[1], parts[2], part)):
            z = z + jnp.where(lane == c * RHS + sub, jnp.sum(val, axis=1, keepdims=True), 0.0)
        msg = jnp.concatenate([jnp.zeros((RHS, BS), f32), jnp.sum(z, axis=0, keepdims=True)], 0)

        def put(j):
            send[pl.ds(rows * j, rows), :] = msg

        each(NDEV, put)
    for b in range(2):
        for k in range(KMAX):
            used, dev, _ = slots[b][k]

            @pl.when(used)
            def _():
                at = pl.ds(rows * dev, RHS)
                send[at, :] = send[at, :] + backs[b][:, k * BS : (k + 1) * BS]


def returned(rows, recv0, recv):
    def step(j, acc):
        flag = recv0[pl.ds(5 * j + 4, 1), :]
        msg = recv[pl.ds(rows * j, RHS), :]
        out = [a + jnp.where(flag == float(w), msg, 0.0) for w, a in enumerate(acc[:2])]
        if rows > RHS:
            out.append(acc[2] + recv[pl.ds(rows * j + RHS, 1), :])
        return tuple(out)

    init = (jnp.zeros((RHS, BS), f32), jnp.zeros((RHS, BS), f32))
    if rows > RHS:
        init = init + (jnp.zeros((1, BS), f32),)
    return lax.fori_loop(0, NDEV, step, init, unroll=8)


def middle_body(recv0, recv, q, d0, args, gd, apart, im0, y, parts, send):
    ret = returned(RHS, recv0, recv)
    rz = jnp.zeros((RHS, BS), f32)
    bb = jnp.zeros((RHS, BS), f32)
    ys = []
    for b in range(2):
        s = slice(b * BS, (b + 1) * BS)
        d = d0[b]
        im = q[b] + ret[b] + args[2:3, s] * d
        dn = 1.0 / args[2:3, s]
        w = im * dn
        yb = w - mm(mm_nt(w, gd[b]), gd[b]) * dn
        im0[b] = im
        y[b] = yb
        ys.append(yb)
        bb = bb + im * yb
        rz = rz + args[8:24, s] * d
    parts[0] = rz
    parts[1] = apart[...]
    parts[2] = bb

    def put(j):
        flag = recv0[pl.ds(5 * j + 4, 1), :]
        send[pl.ds(pl.multiple_of(RHS * j, RHS), RHS), :] = jnp.where(flag == 1.0, ys[1], ys[0])

    each(NDEV, put)


def last_body(recv0, recv, q1, y, d0, im0, args, sol, res):
    ret = returned(RHS + 1, recv0, recv)
    lane = lax.broadcasted_iota(jnp.int32, (RHS, BS), 1)
    sub = lax.broadcasted_iota(jnp.int32, (RHS, BS), 0)
    rz, a, bb, cc = [
        jnp.sum(jnp.where(lane == c * RHS + sub, ret[2], 0.0), axis=1, keepdims=True) for c in range(4)
    ]
    al0 = rz / a
    new = al0 * al0 * bb - rz
    grow = 1.0 + new / rz
    al1 = new / (al0 * al0 * cc - grow * grow * a)
    for b in range(2):
        s = slice(b * BS, (b + 1) * BS)
        w = q1[b] + ret[b] + args[2:3, s] * y[b]
        sol[:, s] = al0 * d0[b] + al1 * (grow * d0[b] - al0 * y[b])
        res[:, s] = args[8:24, s] - al0 * im0[b] - al1 * (grow * im0[b] - al0 * w)


def per_device(locations, neighbors, noise_precision, right_side):
    blk = (2, RHS, BS)
    sq = (2, BS, BS)

    def exchange(msg, rows):
        out = lax.all_to_all(msg.reshape(NDEV, 1, rows * BS), "blk", 0, 0, tiled=True)
        return out.reshape(NDEV * rows, BS)

    hbm = pl.BlockSpec(memory_space=pltpu.HBM)
    smem = pltpu.SMEM((2, KMAX), jnp.int32)
    send0, own0 = pl.pallas_call(
        announce_body,
        in_specs=[hbm] * 4,
        out_specs=[VM] * 2,
        out_shape=[jax.ShapeDtypeStruct(s, f32) for s in ((NDEV * 5, BS), (24, 2 * BS))],
        scratch_shapes=[smem, pltpu.SemaphoreType.DMA((4,))],
        name="announce",
    )(neighbors.T, locations, noise_precision.reshape(1, 2 * BS), right_side)
    recv0 = exchange(send0, 5)
    shapes = [(2, BS, KMAX * BS), sq, sq, blk, (NDEV * RHS, BS), (24, 2 * BS)]
    fac, g4, gd, d0, send1, own, nbr = pl.pallas_call(
        factor_body,
        in_specs=[hbm, VM, hbm],
        out_specs=[VM] * 7,
        out_shape=[jax.ShapeDtypeStruct(s, f32) for s in shapes] + [jax.ShapeDtypeStruct((2, KMAX), jnp.int32)],
        scratch_shapes=[
            pltpu.VMEM((2, 640, 640), f32),
            pltpu.VMEM((4, BS, BS), f32),
            pltpu.VMEM((4, 2, BS, BS), f32),
            pltpu.VMEM((2, BS, KMAX * BS), f32),
            smem,
            pltpu.SemaphoreType.DMA((3,)),
        ],
        compiler_params=pltpu.CompilerParams(vmem_limit_bytes=32 * 2**20),
        name="factor",
    )(neighbors.T, recv0, own0)
    recv1 = exchange(send1, RHS)
    q0, apart, send2 = call(
        lambda *r: apply_body(RHS, *r), [blk, (RHS, BS), (NDEV * RHS, BS)], 6, smem=1, name="apply_first"
    )(nbr, d0, recv1, fac, g4, own)
    recv2 = exchange(send2, RHS)
    im0, y, parts, send3 = call(
        middle_body, [blk, blk, (3, RHS, BS), (NDEV * RHS, BS)], 7, name="middle"
    )(recv0, recv2, q0, d0, own, gd, apart)
    recv3 = exchange(send3, RHS)
    q1, send4 = call(
        lambda *r: apply_body(RHS + 1, *r), [blk, (NDEV * (RHS + 1), BS)], 7, smem=1, name="apply_second"
    )(nbr, y, recv3, fac, g4, own, parts)
    recv4 = exchange(send4, RHS + 1)
    return tuple(
        call(last_body, [(RHS, 2 * BS)] * 2, 7, name="last")(
            recv0, recv4, q1, y, d0, im0, own
        )
    )


def solution(mesh):
    in_specs = (P(None, "blk"), P(None, "blk"), P("blk"), P(None, "blk"))
    out_specs = (P(None, "blk"), P(None, "blk"))
    return jax.shard_map(
        per_device, mesh=mesh, in_specs=in_specs, out_specs=out_specs, check_vma=False
    )
```

```python
import jax
import jax.numpy as jnp
from jax import lax
from jax.experimental import pallas as pl
from jax.experimental.pallas import tpu as pltpu
from jax.sharding import PartitionSpec as P

BS = 128
KMAX = 4
RHS = 16
NDEV = 128
f32 = jnp.float32
HI = lax.Precision.HIGHEST
VM = pl.BlockSpec(memory_space=pltpu.VMEM)
SM = pl.BlockSpec(memory_space=pltpu.SMEM)


def call(body, shapes, n_in, scratch=(), name=None, smem=0, limit=32):
    return pl.pallas_call(
        body,
        in_specs=[SM] * smem + [VM] * (n_in - smem),
        out_specs=[VM] * len(shapes),
        out_shape=[jax.ShapeDtypeStruct(s, f32) for s in shapes],
        scratch_shapes=list(scratch),
        compiler_params=pltpu.CompilerParams(vmem_limit_bytes=limit * 2**20),
        name=name,
    )


def dg(a,b,ca,cb):
    return lax.dot_general(a,b,(((ca,),(cb,)),((),())),precision=HI,preferred_element_type=f32)
def mm(a,b): return dg(a,b,1,0)
def mm_nt(a,b): return dg(a,b,1,1)
def split(a):
    hi=a.astype(jnp.bfloat16)
    return hi,(a-hi.astype(f32)).astype(jnp.bfloat16)
def dot3(a,hi,lo,cb):
    ah,al=split(a)
    def one(x,y): return lax.dot_general(x,y,(((1,),(cb,)),((),())),preferred_element_type=f32)
    return one(ah,hi)+(one(ah,lo)+one(al,hi))
def mm_tn(a,b): return dg(a,b,0,0)

def chol_pieces(T, ms, put, SP=64):
    lane=lax.broadcasted_iota(jnp.int32,(8,128),1)
    sub=lax.broadcasted_iota(jnp.int32,(8,128),0)
    NP=SP//8
    for s in range(0,128,SP):
        fin=[[None]*NP for _ in ms]
        R=[[T[m,s+8*q:s+8*q+8,:] for q in range(NP)] for m in ms]
        for q in range(NP):
            base=s+8*q
            inblk=(lane>=base)&(lane<base+8)
            for n in range(len(ms)):
                W=R[n][q]
                C=[jnp.broadcast_to(jnp.sum(jnp.where(lane==base+j,W,0.0),axis=1,keepdims=True),(8,128)) for j in range(8)]
                F=W
                for j in range(8):
                    at=lane==base+j; row=sub==j
                    d=jnp.broadcast_to(C[j][j:j+1],(8,128))
                    r=1.0/d
                    unit=jnp.where(at,1.0,jnp.broadcast_to(W[j:j+1],(8,128)))
                    F=jnp.where(row,unit*lax.rsqrt(d),F)
                    if q<NP-1:
                        pr=unit*r
                        W=jnp.where(row,pr,jnp.where(at,0.0,W)-C[j]*pr)
                        ls=range(j+1,8)
                    else:
                        mul=jnp.where(sub>j,C[j]*r,0.0)
                        W=jnp.where(at&(sub>j),0.0,W)-mul*unit
                        ls=range(j+1,8)
                    for l in ls:
                        e=jnp.broadcast_to(C[l][j:j+1],(8,128))*r
                        C[l]=C[l]-C[j]*e if q==NP-1 else jnp.where(row,e,C[l]-C[j]*e)
                fin[n][q]=F
                put(ms[n],base,jnp.where(lane<=sub+base,F,0.0))
                if q<NP-1:
                    Yr=[jnp.broadcast_to(W[j:j+1],(8,128)) for j in range(8)]
                    for o in range(q+1,NP):
                        A=R[n][o]
                        t=[jnp.broadcast_to(jnp.sum(jnp.where(lane==base+j,A,0.0),axis=1,keepdims=True),(8,128))*Yr[j] for j in range(8)]
                        acc=jnp.where(inblk,0.0,A)-(((t[0]+t[1])+(t[2]+t[3]))+((t[4]+t[5])+(t[6]+t[7])))
                        R[n][o]=acc
            yield
        if s+SP<128:
            lane2=lax.broadcasted_iota(jnp.int32,(128-s-SP,128),1)
            ins=(lane2>=s)&(lane2<s+SP)
            for n,m in enumerate(ms):
                F=jnp.concatenate(fin[n],0)
                own=s+lax.broadcasted_iota(jnp.int32,(SP,128),0)
                lf=lax.broadcasted_iota(jnp.int32,(SP,128),1)
                F2=jnp.where((lf<=own)|(lf>=s+SP),F,0.0)
                T[m,s+SP:,:]=jnp.where(ins,0.0,T[m,s+SP:,:])-mm(jnp.transpose(F)[s+SP:],F2)
            yield

def chol_inverse(T, ms, put, fill=(), pieces=17):
    fill=list(fill)
    for i,_ in enumerate(chol_pieces(T,ms,put)):
        take=-(-len(fill)//max(pieces-i,1))
        for f in fill[:take]: f()
        fill=fill[take:]
    for f in fill: f()

def cov(xc,yc,xr,yr):
    dx=xc-xr; dy=yc-yr
    return jnp.exp(jnp.sqrt(dx*dx+dy*dy)*(-2.5))

def slot(nbr,k,b):
    ident=nbr[b,k]; used=ident>=0; safe=jnp.where(used,ident,0)
    return used,safe//2,safe%2

def factor_body(nbr_hbm, recv0, own_hbm, fac_hi, fac_lo, g4, gd, d0, send, own, nbr_v, X, T, G, coef, nbr, sems):
    pairs=[(nbr_hbm,nbr),(own_hbm,own),(nbr_hbm,nbr_v)]
    copies=[pltpu.make_async_copy(a,b,sems.at[i]) for i,(a,b) in enumerate(pairs)]
    for c in copies: c.start()
    for c in copies: c.wait()
    i0=lax.broadcasted_iota(jnp.int32,(128,128),0); i1=lax.broadcasted_iota(jnp.int32,(128,128),1)
    eye=jnp.where(i0==i1,1.0,0.0).astype(f32)
    early=[]
    for b in range(2):
        xs=[];ys=[];ms=[]
        for k in range(4):
            used,dev,which=slot(nbr,k,b)
            xs.append(recv0[pl.ds(5*dev+which,1),:]); ys.append(recv0[pl.ds(5*dev+which+2,1),:])
            ms.append(jnp.where(used,1.0,0.0).astype(f32))
        xs.append(own[0:1,b*128:(b+1)*128]); ys.append(own[1:2,b*128:(b+1)*128]); ms.append(jnp.float32(1.0))
        xt=jnp.transpose(jnp.concatenate(xs+[xs[4]]*3,0)); yt=jnp.transpose(jnp.concatenate(ys+[ys[4]]*3,0))
        def block(k,l,b=b,xs=xs,ys=ys,ms=ms,xt=xt,yt=yt):
            xc=jnp.broadcast_to(xt[:,k:k+1],(128,128)); yc=jnp.broadcast_to(yt[:,k:k+1],(128,128))
            c=cov(xc,yc,xs[l],ys[l])
            if k<4 or l<4: c=c*(ms[k]*ms[l])
            if k==l: c=c+eye*(0.2*ms[k]+1.0-ms[k])
            if k==0: T[b]=c
            else: X[b,k*128:(k+1)*128,l*128:(l+1)*128]=c
        block(0,0)
        for k in range(1,5):
            for l in range(k+1):
                early.append(lambda k=k,l=l,block=block: block(k,l))
    def at(i,j): return (slice(i*128,(i+1)*128),slice(j*128,(j+1)*128))
    fill=early
    for k in range(4):
        def put(m,row,v,k=k): G[k,m,row:row+8,:]=v
        chol_inverse(T,[0,1],put,fill)
        fill=[]
        n=k+1
        for b in range(2):
            r,c=at(n,k)
            L=mm_nt(X[b,r,c],G[k,b])
            X[b,r,c]=L
            r,c=at(n,n)
            T[b]=X[b,r,c]-mm_nt(L,L)
        for b in range(2):
            lo=(n+1)*128
            if n<4:
                X[b,lo:,k*128:n*128]=mm_nt(X[b,lo:,k*128:n*128],G[k,b])
                for j in range(n,5):
                    o=max(j,n+1)*128
                    c=slice(k*128,n*128)
                    X[b,o:,j*128:(j+1)*128]=X[b,o:,j*128:(j+1)*128]-mm_nt(X[b,o:,c],X[b,j*128:(j+1)*128,c])
    dn=[]
    for b in range(2):
        d=1.0/own[2:3,b*128:(b+1)*128]; dn.append(d)
        T[2+b]=T[b]+eye*d
    def put4(m,row,v):
        if m<2: g4[m,row:row+8,:]=v
        else: gd[m-2,row:row+8,:]=v
    for k in (3,2,1,0):
        for b in range(2):
            def term(b=b,k=k):
                X[b,512:,k*128:(k+1)*128]=X[b,512:,k*128:(k+1)*128]-mm(coef[b,:,(k+1)*128:],X[b,(k+1)*128:512,k*128:(k+1)*128])
            def close(b=b,k=k):
                coef[b,:,k*128:(k+1)*128]=mm(X[b,512:,k*128:(k+1)*128],G[k,b])
            if k<3: fill.append(term)
            fill.append(close)
    chol_inverse(T,[0,1,2,3],put4,fill)
    ds=[]
    for b in range(2):
        fac_hi[b],fac_lo[b]=split(mm(g4[b],coef[b]))
        w=own[8:24,b*128:(b+1)*128]*dn[b]
        d=w-mm(mm_nt(w,gd[b]),gd[b])*dn[b]
        d0[b]=d
        ds.append(d)
    def pack(j,_):
        flag=recv0[pl.ds(5*j+4,1),:]
        send[pl.ds(pl.multiple_of(RHS*j,RHS),RHS),:]=jnp.where(flag==1.0,ds[1],ds[0])
        return 0
    lax.fori_loop(0,NDEV,pack,0,unroll=8)


def each(n, body, unroll=8):
    def step(j, carry):
        body(j)
        return carry

    lax.fori_loop(0, n, step, 0, unroll=unroll)


def announce_body(nbr_hbm, loc_hbm, noise_hbm, rhs_hbm, out, own, nbr, sems):
    pairs = [(nbr_hbm, nbr), (loc_hbm, own.at[0:2]), (noise_hbm, own.at[2:3]), (rhs_hbm, own.at[8:24])]
    copies = [pltpu.make_async_copy(s, d, sems.at[i]) for i, (s, d) in enumerate(pairs)]
    own[...] = jnp.zeros((24, 2 * BS), f32)
    for c in copies:
        c.start()
    for c in copies:
        c.wait()
    loc = own[0:2, :]
    rows = jnp.concatenate(
        [loc[0:1, 0:BS], loc[0:1, BS:], loc[1:2, 0:BS], loc[1:2, BS:], jnp.full((1, BS), -1.0, f32)], 0
    )

    def put(j):
        out[pl.ds(5 * j, 5), :] = rows

    each(NDEV, put)
    for b in range(2):
        for k in range(KMAX):
            used, dev, which = slot(nbr, k, b)

            @pl.when(used)
            def _():
                out[pl.ds(5 * dev + 4, 1), :] = jnp.full((1, BS), which.astype(f32), f32)


def apply_body(rows, nbr, v, recv, fac_hi, fac_lo, g4, args, *rest):
    if rows == RHS:
        q_out, part_out, send = rest
        send[...] = jnp.zeros((NDEV * RHS, BS), f32)
    else:
        parts, q_out, send = rest
    part = jnp.zeros((RHS, BS), f32)
    backs = []
    slots = [[slot(nbr, k, b) for k in range(KMAX)] for b in range(2)]
    for b in range(2):
        near = jnp.concatenate([recv[pl.ds(pl.multiple_of(RHS * s[1], 8), RHS), :] for s in slots[b]], 1)
        own = v[b]
        t = mm_nt(own, g4[b]) - dot3(near, fac_hi[b], fac_lo[b], 1)
        q = mm(t, g4[b])
        part = part + t * t + args[2:3, b * BS : (b + 1) * BS] * own * own
        q_out[b] = q
        backs.append(-dot3(t, fac_hi[b], fac_lo[b], 0))
    if rows == RHS:
        part_out[...] = part
    else:
        lane = lax.broadcasted_iota(jnp.int32, (RHS, BS), 1)
        sub = lax.broadcasted_iota(jnp.int32, (RHS, BS), 0)
        z = jnp.zeros((RHS, BS), f32)
        for c, val in enumerate((parts[0], parts[1], parts[2], part)):
            z = z + jnp.where(lane == c * RHS + sub, jnp.sum(val, axis=1, keepdims=True), 0.0)
        msg = jnp.concatenate([jnp.zeros((RHS, BS), f32), jnp.sum(z, axis=0, keepdims=True)], 0)

        def put(j):
            send[pl.ds(rows * j, rows), :] = msg

        each(NDEV, put)
    for b in range(2):
        for k in range(KMAX):
            used, dev, _ = slots[b][k]

            @pl.when(used)
            def _():
                at = pl.ds(rows * dev, RHS)
                send[at, :] = send[at, :] + backs[b][:, k * BS : (k + 1) * BS]


def returned(rows, recv0, recv):
    def step(j, acc):
        flag = recv0[pl.ds(5 * j + 4, 1), :]
        msg = recv[pl.ds(rows * j, RHS), :]
        out = [a + jnp.where(flag == float(w), msg, 0.0) for w, a in enumerate(acc[:2])]
        if rows > RHS:
            out.append(acc[2] + recv[pl.ds(rows * j + RHS, 1), :])
        return tuple(out)

    init = (jnp.zeros((RHS, BS), f32), jnp.zeros((RHS, BS), f32))
    if rows > RHS:
        init = init + (jnp.zeros((1, BS), f32),)
    return lax.fori_loop(0, NDEV, step, init, unroll=8)


def middle_body(recv0, recv, q, d0, args, gd, apart, im0, y, parts, send):
    ret = returned(RHS, recv0, recv)
    rz = jnp.zeros((RHS, BS), f32)
    bb = jnp.zeros((RHS, BS), f32)
    ys = []
    for b in range(2):
        s = slice(b * BS, (b + 1) * BS)
        d = d0[b]
        im = q[b] + ret[b] + args[2:3, s] * d
        dn = 1.0 / args[2:3, s]
        w = im * dn
        yb = w - mm(mm_nt(w, gd[b]), gd[b]) * dn
        im0[b] = im
        y[b] = yb
        ys.append(yb)
        bb = bb + im * yb
        rz = rz + args[8:24, s] * d
    parts[0] = rz
    parts[1] = apart[...]
    parts[2] = bb

    def put(j):
        flag = recv0[pl.ds(5 * j + 4, 1), :]
        send[pl.ds(pl.multiple_of(RHS * j, RHS), RHS), :] = jnp.where(flag == 1.0, ys[1], ys[0])

    each(NDEV, put)


def last_body(recv0, recv, q1, y, d0, im0, args, sol, res):
    ret = returned(RHS + 1, recv0, recv)
    lane = lax.broadcasted_iota(jnp.int32, (RHS, BS), 1)
    sub = lax.broadcasted_iota(jnp.int32, (RHS, BS), 0)
    rz, a, bb, cc = [
        jnp.sum(jnp.where(lane == c * RHS + sub, ret[2], 0.0), axis=1, keepdims=True) for c in range(4)
    ]
    al0 = rz / a
    new = al0 * al0 * bb - rz
    grow = 1.0 + new / rz
    al1 = new / (al0 * al0 * cc - grow * grow * a)
    for b in range(2):
        s = slice(b * BS, (b + 1) * BS)
        w = q1[b] + ret[b] + args[2:3, s] * y[b]
        sol[:, s] = al0 * d0[b] + al1 * (grow * d0[b] - al0 * y[b])
        res[:, s] = args[8:24, s] - al0 * im0[b] - al1 * (grow * im0[b] - al0 * w)


def per_device(locations, neighbors, noise_precision, right_side):
    blk = (2, RHS, BS)
    sq = (2, BS, BS)

    def exchange(msg, rows):
        out = lax.all_to_all(msg.reshape(NDEV, 1, rows * BS), "blk", 0, 0, tiled=True)
        return out.reshape(NDEV * rows, BS)

    hbm = pl.BlockSpec(memory_space=pltpu.HBM)
    smem = pltpu.SMEM((2, KMAX), jnp.int32)
    send0, own0 = pl.pallas_call(
        announce_body,
        in_specs=[hbm] * 4,
        out_specs=[VM] * 2,
        out_shape=[jax.ShapeDtypeStruct(s, f32) for s in ((NDEV * 5, BS), (24, 2 * BS))],
        scratch_shapes=[smem, pltpu.SemaphoreType.DMA((4,))],
        name="announce",
    )(neighbors.T, locations, noise_precision.reshape(1, 2 * BS), right_side)
    recv0 = exchange(send0, 5)
    wide = jax.ShapeDtypeStruct((2, BS, KMAX * BS), jnp.bfloat16)
    shapes = [sq, sq, blk, (NDEV * RHS, BS), (24, 2 * BS)]
    fac_hi, fac_lo, g4, gd, d0, send1, own, nbr = pl.pallas_call(
        factor_body,
        in_specs=[hbm, VM, hbm],
        out_specs=[VM] * 8,
        out_shape=[wide, wide]
        + [jax.ShapeDtypeStruct(s, f32) for s in shapes]
        + [jax.ShapeDtypeStruct((2, KMAX), jnp.int32)],
        scratch_shapes=[
            pltpu.VMEM((2, 640, 640), f32),
            pltpu.VMEM((4, BS, BS), f32),
            pltpu.VMEM((4, 2, BS, BS), f32),
            pltpu.VMEM((2, BS, KMAX * BS), f32),
            smem,
            pltpu.SemaphoreType.DMA((3,)),
        ],
        compiler_params=pltpu.CompilerParams(vmem_limit_bytes=32 * 2**20),
        name="factor",
    )(neighbors.T, recv0, own0)
    recv1 = exchange(send1, RHS)
    q0, apart, send2 = call(
        lambda *r: apply_body(RHS, *r), [blk, (RHS, BS), (NDEV * RHS, BS)], 7, smem=1, name="apply_first"
    )(nbr, d0, recv1, fac_hi, fac_lo, g4, own)
    recv2 = exchange(send2, RHS)
    im0, y, parts, send3 = call(
        middle_body, [blk, blk, (3, RHS, BS), (NDEV * RHS, BS)], 7, name="middle"
    )(recv0, recv2, q0, d0, own, gd, apart)
    recv3 = exchange(send3, RHS)
    q1, send4 = call(
        lambda *r: apply_body(RHS + 1, *r), [blk, (NDEV * (RHS + 1), BS)], 8, smem=1, name="apply_second"
    )(nbr, y, recv3, fac_hi, fac_lo, g4, own, parts)
    recv4 = exchange(send4, RHS + 1)
    return tuple(
        call(last_body, [(RHS, 2 * BS)] * 2, 7, name="last")(
            recv0, recv4, q1, y, d0, im0, own
        )
    )


def solution(mesh):
    in_specs = (P(None, "blk"), P(None, "blk"), P("blk"), P(None, "blk"))
    out_specs = (P(None, "blk"), P(None, "blk"))
    return jax.shard_map(
        per_device, mesh=mesh, in_specs=in_specs, out_specs=out_specs, check_vma=False
    )
```
